32 devices in a mesh: cls: 4 (over z), site: 8 (over y, x, core).
Axes of the slice: x: 2, y: 2, z: 4, core: 2. Of those that a mesh axis runs over, the one named last changes fastest.
Arguments:
- tip_codes: int32 [1024, 8192], P('cls', 'site'), may hold values from 0 to 3
- counts: int32 [8192], P('site'), may hold values from 1 to 5
- children: int32 [1023, 2], replicated, may hold values from 0 to 2045, as said below
- lengths: float32 [4, 2046], replicated, may hold values from 0.01 to 1
- frequencies: float32 [4, 4], replicated, may hold values from 0.25 to 1.75
- weights: float32 [4], replicated, may hold values from 0.2 to 1
Outputs:
- site_loglik: float32 [4, 2048], P('cls', 'site')
- new_weights: float32 [4], P('cls')
- mean_loglik: float32 [], replicated
The draws below stay inside these ranges and needn't reach their ends.
Inputs may be any that keep to these rules, and one draw needn't show every extreme that they name: Row k lists the two children of internal node 1024 + k as node ids. Give the tips height 0 and the root height 10. The nodes of height h + 1 have exactly the nodes of height h as children, each once, and the root is node 2046. For every height h from 0 to 5, split the parents (height h + 1) and the children (height h) into 16 equal aligned blocks: the children of parent block j are child block j, so the tips j * 64 onward form clade j.
All inputs are finite; a program needn't handle non-finite values.
Results may differ from the reference program's by a relative error of at most 0.0003.
Values sent between devices are 32-bit elements; how exact they have to be, the bound alone decides.
A program may use at most 64 MiB of HBM per device.

```python
import math
import jax
import jax.numpy as jnp
from jax import lax

LEVELS = 10
TOP = 4
CLS = 4
SITE_DEV = 1024
TAXA = 1024
BRANCHES = 2046
SITES = 8192
N_SITE = 8


def draw_children(key, part):
    pieces = []
    for tree_level in range(LEVELS):
        level_below = TAXA >> tree_level
        if tree_level == 0:
            first_id = 0
        else:
            first_id = TAXA + TAXA - (TAXA >> tree_level - 1)
        if tree_level < LEVELS - TOP:
            blocks = 2 ** TOP
        else:
            blocks = 1
        block_size = level_below // blocks
        level_key = jax.random.fold_in(key, 17 + tree_level)
        block_keys = jax.random.split(level_key, blocks)
        shuffled = jax.vmap(lambda one_key: jax.random.permutation(one_key, block_size))(block_keys)
        shuffled = shuffled.astype(jnp.int32) + (jnp.arange(blocks, dtype=jnp.int32) * block_size)[:, None]
        pieces.append((shuffled.reshape(level_below // 2, 2) + first_id).astype(jnp.int32))
    return jnp.concatenate(pieces, axis=0)


def draw_counts(key, part):
    position = jnp.arange(SITES, dtype=jnp.int32)
    upper_end = 2 + 5 * position // SITES
    return jax.random.randint(jax.random.fold_in(key, 5), (SITES,), 1, upper_end, dtype=jnp.int32)


def with_ends(values, own_key, low, high):
    dims = values.shape
    spot = [jax.random.randint(jax.random.fold_in(own_key, axis), (), 0, dims[axis]) for axis in range(len(dims))]
    values = values.at[tuple(spot)].set(low)
    longest = dims.index(max(dims))
    spot[longest] = (spot[longest] + 1) % dims[longest]
    return values.at[tuple(spot)].set(high)


def setup_inputs(seed: int = 0) -> dict:
    keys = jax.random.split(jax.random.key(seed), 7)
    return {
        "tip_codes": with_ends(jax.random.randint(keys[0], (TAXA, SITES), 0, 4), jax.random.fold_in(keys[0], 1), 0, 3).astype(jnp.int32),
        "counts": draw_counts(jax.random.fold_in(keys[6], 71), 0),
        "children": draw_children(jax.random.fold_in(keys[6], 71), 0),
        "lengths": jnp.clip(jnp.exp(jax.random.uniform(keys[3], (CLS, BRANCHES), jnp.float32, math.log(0.01), math.log(1.0))), 0.01, 1.0),
        "frequencies": jnp.clip(1.0 + 0.15 * jax.random.normal(keys[4], (CLS, 4), jnp.float32), 0.25, 1.75),
        "weights": jnp.clip(jnp.exp(jax.random.uniform(keys[5], (CLS,), jnp.float32, math.log(0.2), math.log(1.0))), 0.2, 1.0),
    }


def transit(values, decays, stationary):
    average = jnp.sum(stationary[None, :, None] * values, axis=1, keepdims=True)
    return decays[:, None, None] * values + (1.0 - decays)[:, None, None] * average


def from_codes(codes, decays, stationary):
    states = jnp.arange(4, dtype=jnp.int32)
    onehot = (codes[:, None, :] == states[None, :, None]).astype(jnp.float32)
    return transit(onehot, decays, stationary)


def join_pair(left_part, right_part, scale_sum):
    parent = left_part * right_part
    largest = jnp.max(parent, axis=1, keepdims=True)
    return parent / largest, scale_sum + jnp.log(largest)


def class_loglik(tip_block, children, length_row, stationary):
    rate_scale = 1.0 / (1.0 - jnp.sum(stationary * stationary))
    values = None
    scales = None
    for tree_level in range(LEVELS):
        node_count = TAXA >> (tree_level + 1)
        offset = TAXA - (TAXA >> tree_level)
        child_ids = children[offset:offset + node_count]
        left_ids = child_ids[:, 0]
        right_ids = child_ids[:, 1]
        left_decay = jnp.exp(-rate_scale * length_row[left_ids])
        right_decay = jnp.exp(-rate_scale * length_row[right_ids])
        if tree_level == 0:
            left_part = from_codes(tip_block[left_ids], left_decay, stationary)
            right_part = from_codes(tip_block[right_ids], right_decay, stationary)
            scale_sum = jnp.zeros((node_count, 1, tip_block.shape[1]), jnp.float32)
        else:
            anchor = TAXA + TAXA - (TAXA >> (tree_level - 1))
            left_rows = (left_ids - anchor).astype(jnp.int32)
            right_rows = (right_ids - anchor).astype(jnp.int32)
            left_part = transit(values[left_rows], left_decay, stationary)
            right_part = transit(values[right_rows], right_decay, stationary)
            scale_sum = scales[left_rows] + scales[right_rows]
        values, scales = join_pair(left_part, right_part, scale_sum)
    return scales[0, 0] + jnp.log(jnp.sum(stationary[:, None] * values[0], axis=0))


def reference(tip_codes, counts, children, lengths, frequencies, weights):
    stationary = frequencies / jnp.sum(frequencies, axis=1, keepdims=True)
    log_weight = jnp.log(weights / jnp.sum(weights))
    block_count = SITES // SITE_DEV
    tip_blocks = tip_codes.reshape(TAXA, block_count, SITE_DEV).transpose(1, 0, 2)

    def one_block(tip_block):
        return jnp.stack([class_loglik(tip_block, children, lengths[class_no], stationary[class_no]) for class_no in range(CLS)])

    per_class = lax.map(one_block, tip_blocks)
    per_class = per_class.transpose(1, 0, 2).reshape(CLS, SITES)
    shifted = per_class + log_weight[:, None]
    largest = jnp.max(shifted, axis=0)
    site_total = largest + jnp.log(jnp.sum(jnp.exp(shifted - largest[None, :]), axis=0))
    posterior = jnp.exp(shifted - site_total[None, :])
    pattern_weight = counts.astype(jnp.float32)
    class_mass = jnp.sum(pattern_weight[None, :] * posterior, axis=1)
    all_count = jnp.sum(pattern_weight)
    new_weights = class_mass / all_count
    mean_loglik = jnp.sum(pattern_weight * site_total) / (all_count * TAXA)
    per_taxon = (site_total / TAXA).reshape(N_SITE, CLS, SITE_DEV // CLS).transpose(1, 0, 2).reshape(CLS, SITES // CLS)
    return per_taxon, new_weights, mean_loglik
```

```python
import functools

import jax
import jax.numpy as jnp
from jax import lax
from jax.experimental import pallas as pl
from jax.experimental.pallas import tpu as pltpu
from jax.sharding import PartitionSpec as P

LEVELS = 10
TOP = 4
LANES = 128
MESH = pl.DeviceIdType.MESH


def level_base(taxa, h):
    return 0 if h == 0 else 2 * taxa - (taxa >> (h - 1))


def kernel(
    groups,
    site_devices,
    codes_hbm,
    counts_ref,
    kids_ref,
    kids_smem,
    lengths_ref,
    freq_ref,
    weights_ref,
    site_out,
    weight_out,
    mean_out,
    codes,
    picked,
    table,
    grow,
    grow_up,
    stat,
    sent,
    got,
    upper,
    part,
    part_got,
    group_sum,
    group_got,
    code_sem,
    send_sem,
    recv_sem,
    part_send,
    part_recv,
    sum_send,
    sum_recv,
):
    g = lax.axis_index("cls")
    me = lax.axis_index("site")
    local, sites = codes_hbm.shape
    taxa = local * groups
    classes, branches = lengths_ref.shape
    quarter = sites // groups
    halves = quarter // LANES
    low = LEVELS - TOP
    clades = local >> low
    rows = halves * classes
    f32 = jnp.float32
    bf16 = jnp.bfloat16

    fetch = pltpu.make_async_copy(codes_hbm, codes, code_sem)
    fetch.start()

    barrier = pltpu.get_barrier_semaphore()
    for k in range(1, groups):
        pl.semaphore_signal(
            barrier, inc=1, device_id={"cls": lax.rem(g + k, groups)}, device_id_type=MESH
        )
    for k in range(1, site_devices):
        pl.semaphore_signal(
            barrier,
            inc=1,
            device_id={"site": lax.rem(me + k, site_devices)},
            device_id_type=MESH,
        )

    freq = freq_ref[...]
    pi = freq / jnp.sum(freq, axis=1, keepdims=True)
    beta = 1.0 / (1.0 - jnp.sum(pi * pi, axis=1, keepdims=True))
    lengths = lengths_ref[...]
    r = jnp.exp(beta * lengths) - 1.0
    drift = beta * jnp.sum(lengths, axis=1, keepdims=True)

    table[...] = jnp.zeros_like(table)
    hi = r.astype(bf16).astype(f32)
    rest = r - hi
    mid = rest.astype(bf16).astype(f32)
    table[0:classes, 0:branches] = hi
    table[classes : 2 * classes, 0:branches] = mid
    table[2 * classes : 3 * classes, 0:branches] = rest - mid
    kids = kids_ref[...]
    table[12:14, taxa : taxa + kids.shape[1]] = (kids >> 8).astype(f32)
    table[14:16, taxa : taxa + kids.shape[1]] = (kids & 255).astype(f32)

    pi8 = jnp.concatenate([pi] * halves, axis=0)
    for c in range(classes):
        for i in range(4):
            wide = jnp.broadcast_to(pi[:, i : i + 1], (classes, LANES))
            stat[c, i] = jnp.broadcast_to(wide[c : c + 1], (8, LANES))
    first_up = level_base(taxa, low)
    window = first_up // LANES * LANES
    r8 = jnp.concatenate([r[:, window:branches]] * halves, axis=0)
    for j in range(branches - first_up):
        at = first_up - window + j
        grow_up[j] = jnp.broadcast_to(r8[:, at : at + 1], (rows, LANES))

    q = lax.broadcasted_iota(jnp.int32, (1, local), 1)
    ancestor = (first_up + g * clades + (q & (clades - 1))).astype(f32)
    offset = {}
    total_rows = 0
    for h in range(low):
        offset[h] = total_rows
        total_rows += local >> h
    for h in range(low, -1, -1):
        count = local >> h
        base = level_base(taxa, h)
        if count % LANES == 0:
            start = pl.multiple_of(base + g * count, LANES)
            width = count
        else:
            start = base // LANES * LANES
            end = base + (taxa >> h)
            width = -(-end // LANES) * LANES - start
        ids = lax.broadcasted_iota(jnp.int32, (width, local), 0) + start
        onehot = (ids.astype(f32) == ancestor).astype(f32).astype(bf16)
        part_table = table[:, pl.ds(start, width)].astype(bf16)
        out = jnp.dot(part_table, onehot, preferred_element_type=f32)
        if h < low:
            r_row = out[0:classes] + out[classes : 2 * classes] + out[2 * classes : 3 * classes]
            r_col = jnp.concatenate([r_row, r_row], axis=0).T
            for c in range(classes):
                grow[c, offset[h] : offset[h] + count, :] = jnp.broadcast_to(
                    r_col[:count, c : c + 1], (count, LANES)
                )
        if h > 0:
            left = out[12:13] * 256.0 + out[14:15]
            right = out[13:14] * 256.0 + out[15:16]
            ancestor = jnp.where((q & count) != 0, right, left)
    tip_col = jnp.broadcast_to(ancestor, (8, local)).T[:, 0:1]
    tip_ids = (lax.broadcasted_iota(jnp.int32, (local, local), 1) + g * local).astype(f32)
    order = (tip_ids == tip_col).astype(f32).astype(bf16)

    fetch.wait()

    def quarter_of(k, dest):
        block = lax.rem(g + k, groups)
        for half in range(halves):
            lanes = pl.ds(pl.multiple_of(block * quarter + half * LANES, LANES), LANES)
            picked[half] = jnp.dot(
                order, codes[:, lanes].astype(f32).astype(bf16), preferred_element_type=f32
            )

        def one(step, carry):
            half = step // classes
            c = lax.rem(step, classes)
            pis = [stat[c, i] for i in range(4)]

            def factor(h, n):
                return grow[c, offset[h] + 8 * n : offset[h] + 8 * n + 8, :]

            def tip(n):
                code = picked[half, 8 * n : 8 * n + 8, :]
                marks = [code == float(i) for i in range(4)]
                own = jnp.where(
                    marks[0], pis[0], jnp.where(marks[1], pis[1], jnp.where(marks[2], pis[2], pis[3]))
                )
                off = factor(0, n) * own
                on = off + 1.0
                return [jnp.where(mark, on, off) for mark in marks]

            def spread(values, scale):
                mean = (values[0] * pis[0] + values[1] * pis[1]) + (
                    values[2] * pis[2] + values[3] * pis[3]
                )
                move = scale * mean
                return [value + move for value in values]

            logs = []

            def node(h, n):
                if h == 0:
                    return tip(n)
                gap = (local >> h) // 8
                left = node(h - 1, n)
                right = node(h - 1, n + gap)
                if h > 1:
                    left = spread(left, factor(h - 1, n))
                    right = spread(right, factor(h - 1, n + gap))
                values = [a * b for a, b in zip(left, right)]
                if h == 3:
                    largest = jnp.maximum(
                        jnp.maximum(values[0], values[1]), jnp.maximum(values[2], values[3])
                    )
                    scale = pl.reciprocal(largest, approx=True)
                    logs.append(jnp.log(scale))
                    values = [value * scale for value in values]
                return values

            values = spread(node(low - 1, 0), factor(low - 1, 0))
            values = [value[0:clades] * value[clades : 2 * clades] for value in values]
            log_sum = jnp.sum(sum(logs[1:], logs[0]), axis=0, keepdims=True)
            log_sum = jnp.sum(jnp.log(values[3]), axis=0, keepdims=True) - log_sum
            inverse = 1.0 / values[3]
            for i in range(3):
                ratio = values[i] * inverse
                for j in range(clades):
                    dest[j * 3 + i, pl.ds(step, 1), :] = ratio[j : j + 1]
            dest[clades * 3, pl.ds(step, 1), :] = log_sum
            return carry

        lax.fori_loop(0, rows, one, 0)

    copies = []
    for place, k in enumerate([2, 1, 3] if groups == 4 else range(1, groups)):
        quarter_of(k, sent.at[k])
        if place == 0:
            pl.semaphore_wait(barrier, groups + site_devices - 2)
        copy = pltpu.make_async_remote_copy(
            src_ref=sent.at[k],
            dst_ref=got.at[k],
            send_sem=send_sem.at[k],
            recv_sem=recv_sem.at[k],
            device_id={"cls": lax.rem(g + k, groups)},
            device_id_type=MESH,
        )
        copy.start()
        copies.append(copy)
    quarter_of(0, got.at[0])
    for copy in copies:
        copy.wait()

    pis8 = [jnp.broadcast_to(pi8[:, i : i + 1], (rows, LANES)) for i in range(4)]
    scales = got[0, clades * 3]
    for k in range(1, groups):
        scales = scales + got[k, clades * 3]

    def child(tree_level, ident):
        if tree_level == low:
            clade = jnp.clip(ident - first_up, 0, 2**TOP - 1)
            k = lax.rem(g + groups - clade // clades, groups)
            row = lax.rem(clade, clades) * 3
            values = [got[k, row + i] for i in range(3)] + [jnp.ones((rows, LANES), f32)]
        else:
            at = jnp.clip(ident - level_base(taxa, low + 1), 0, 2**TOP - 1)
            values = [upper[at, i] for i in range(4)]
        mean = (values[0] * pis8[0] + values[1] * pis8[1]) + (
            values[2] * pis8[2] + values[3] * pis8[3]
        )
        move = grow_up[jnp.clip(ident - first_up, 0, branches - first_up - 1)] * mean
        return [value + move for value in values]

    place = 0
    for tree_level in range(low, LEVELS):
        count = taxa >> (tree_level + 1)
        first = taxa - (taxa >> tree_level)
        for n in range(count):
            left = child(tree_level, kids_smem[0, first + n])
            right = child(tree_level, kids_smem[1, first + n])
            values = [a * b for a, b in zip(left, right)]
            largest = jnp.maximum(
                jnp.maximum(values[0], values[1]), jnp.maximum(values[2], values[3])
            )
            scale = pl.reciprocal(largest, approx=True)
            scales = scales - jnp.log(scale)
            values = [value * scale for value in values]
            if tree_level < LEVELS - 1:
                for i in range(4):
                    upper[place, i] = values[i]
                place += 1
    end = (values[0] * pis8[0] + values[1] * pis8[1]) + (
        values[2] * pis8[2] + values[3] * pis8[3]
    )
    spot = lax.broadcasted_iota(jnp.int32, (classes, classes), 0)
    spot = spot == lax.broadcasted_iota(jnp.int32, (classes, classes), 1)
    weights = jnp.sum(jnp.where(spot, weights_ref[...], 0.0), axis=1, keepdims=True)
    log_weight = jnp.log(weights / jnp.sum(weights, axis=0, keepdims=True))
    bias = jnp.concatenate([log_weight - drift] * halves, axis=0)
    shifted = scales + jnp.log(end) + bias

    mass = jnp.zeros((classes, LANES), f32)
    loglik = jnp.zeros((1, LANES), f32)
    seen = jnp.zeros((1, LANES), f32)
    for half in range(halves):
        a = shifted[half * classes : (half + 1) * classes]
        top = jnp.max(a, axis=0, keepdims=True)
        total = top + jnp.log(jnp.sum(jnp.exp(a - top), axis=0, keepdims=True))
        n = counts_ref[pl.ds(g * halves + half, 1), :].astype(f32)
        site_out[0:1, half * LANES : (half + 1) * LANES] = total / taxa
        mass = mass + n * jnp.exp(a - total)
        loglik = loglik + n * total
        seen = seen + n
    part[...] = jnp.zeros_like(part)
    part[0:classes] = mass
    part[classes : classes + 1] = loglik
    part[classes + 1 : classes + 2] = seen

    copies = []
    for k in range(1, groups):
        copy = pltpu.make_async_remote_copy(
            src_ref=part,
            dst_ref=part_got.at[k],
            send_sem=part_send.at[k],
            recv_sem=part_recv.at[k],
            device_id={"cls": lax.rem(g + k, groups)},
            device_id_type=MESH,
        )
        copy.start()
        copies.append(copy)
    for copy in copies:
        copy.wait()
    part_got[0] = part[...]
    sums = part_got[lax.rem(g + groups, groups)]
    for d in range(1, groups):
        sums = sums + part_got[lax.rem(g + groups - d, groups)]
    group_sum[...] = sums
    copies = []
    for k in range(1, site_devices):
        copy = pltpu.make_async_remote_copy(
            src_ref=group_sum,
            dst_ref=group_got.at[k],
            send_sem=sum_send.at[k],
            recv_sem=sum_recv.at[k],
            device_id={"site": lax.rem(me + k, site_devices)},
            device_id_type=MESH,
        )
        copy.start()
        copies.append(copy)
    for copy in copies:
        copy.wait()
    group_got[0] = sums
    sums = group_got[lax.rem(me + site_devices, site_devices)]
    for d in range(1, site_devices):
        sums = sums + group_got[lax.rem(me + site_devices - d, site_devices)]
    line = jnp.sum(sums, axis=1, keepdims=True)
    all_count = line[classes + 1 : classes + 2]
    mean = line[classes : classes + 1] / (all_count * taxa)
    share = line[0:classes] / all_count
    mine = lax.broadcasted_iota(jnp.int32, (classes, 1), 0) == g
    weight_out[0] = jnp.sum(jnp.where(mine, share, 0.0))
    mean_out[0] = jnp.sum(mean)


def solution(mesh):
    groups = mesh.shape["cls"]
    site_devices = mesh.shape["site"]

    def per_device(tip_codes, counts, children, lengths, frequencies, weights):
        local, sites = tip_codes.shape
        taxa = local * groups
        classes, branches = lengths.shape
        quarter = sites // groups
        halves = quarter // LANES
        rows = halves * classes
        low = LEVELS - TOP
        clades = local >> low
        low_rows = sum(local >> h for h in range(low))
        table_width = -(-(branches + 1) // LANES) * LANES
        up_count = branches - level_base(taxa, low)
        kids = children.T
        vmem = pl.BlockSpec(memory_space=pltpu.VMEM)
        smem = pl.BlockSpec(memory_space=pltpu.SMEM)
        f32 = jnp.float32
        site_loglik, new_weights, mean_loglik = pl.pallas_call(
            functools.partial(kernel, groups, site_devices),
            out_shape=(
                jax.ShapeDtypeStruct((1, quarter), f32),
                jax.ShapeDtypeStruct((1,), f32),
                jax.ShapeDtypeStruct((1,), f32),
            ),
            in_specs=[pl.BlockSpec(memory_space=pl.ANY), vmem, vmem, smem, vmem, vmem, vmem],
            out_specs=(vmem, smem, smem),
            scratch_shapes=[
                pltpu.VMEM((local, sites), jnp.int32),
                pltpu.VMEM((halves, local, LANES), f32),
                pltpu.VMEM((16, table_width), f32),
                pltpu.VMEM((classes, low_rows, LANES), f32),
                pltpu.VMEM((up_count, rows, LANES), f32),
                pltpu.VMEM((classes, 4, 8, LANES), f32),
                pltpu.VMEM((groups, clades * 3 + 1, rows, LANES), f32),
                pltpu.VMEM((groups, clades * 3 + 1, rows, LANES), f32),
                pltpu.VMEM((2 ** TOP, 4, rows, LANES), f32),
                pltpu.VMEM((8, LANES), f32),
                pltpu.VMEM((groups, 8, LANES), f32),
                pltpu.VMEM((8, LANES), f32),
                pltpu.VMEM((site_devices, 8, LANES), f32),
                pltpu.SemaphoreType.DMA,
                pltpu.SemaphoreType.DMA((groups,)),
                pltpu.SemaphoreType.DMA((groups,)),
                pltpu.SemaphoreType.DMA((groups,)),
                pltpu.SemaphoreType.DMA((groups,)),
                pltpu.SemaphoreType.DMA((site_devices,)),
                pltpu.SemaphoreType.DMA((site_devices,)),
            ],
            compiler_params=pltpu.CompilerParams(collective_id=0, has_side_effects=True),
        )(
            tip_codes,
            counts.reshape(sites // LANES, LANES),
            kids,
            kids,
            lengths,
            frequencies,
            weights.reshape(1, classes),
        )
        return site_loglik, new_weights, mean_loglik.reshape(())

    return jax.shard_map(
        per_device,
        mesh=mesh,
        in_specs=(P("cls", "site"), P("site"), P(), P(), P(), P()),
        out_specs=(P("cls", "site"), P("cls"), P()),
        check_vma=False,
    )
```

```python
import functools

import jax
import jax.numpy as jnp
from jax import lax
from jax.experimental import pallas as pl
from jax.experimental.pallas import tpu as pltpu
from jax.sharding import PartitionSpec as P

LEVELS = 10
TOP = 4
LANES = 128
MESH = pl.DeviceIdType.MESH


def level_base(taxa, h):
    return 0 if h == 0 else 2 * taxa - (taxa >> (h - 1))


def kernel(
    groups,
    site_devices,
    codes_hbm,
    counts_ref,
    kids_ref,
    kids_smem,
    lengths_ref,
    freq_ref,
    weights_ref,
    result,
    codes,
    picked,
    table,
    grow,
    grow_up,
    stat,
    sent,
    got,
    upper,
    part,
    part_got,
    group_sum,
    group_got,
    code_sem,
    send_sem,
    recv_sem,
    part_send,
    part_recv,
    sum_send,
    sum_recv,
):
    g = lax.axis_index("cls")
    me = lax.axis_index("site")
    local, sites = codes_hbm.shape
    taxa = local * groups
    classes, branches = lengths_ref.shape
    quarter = sites // groups
    halves = quarter // LANES
    low = LEVELS - TOP
    clades = local >> low
    rows = halves * classes
    f32 = jnp.float32
    bf16 = jnp.bfloat16

    fetch = pltpu.make_async_copy(codes_hbm, codes, code_sem)
    fetch.start()

    barrier = pltpu.get_barrier_semaphore()
    for k in range(1, groups):
        pl.semaphore_signal(
            barrier, inc=1, device_id={"cls": lax.rem(g + k, groups)}, device_id_type=MESH
        )
    for k in range(1, site_devices):
        pl.semaphore_signal(
            barrier,
            inc=1,
            device_id={"site": lax.rem(me + k, site_devices)},
            device_id_type=MESH,
        )

    freq = freq_ref[...]
    pi = freq / jnp.sum(freq, axis=1, keepdims=True)
    beta = 1.0 / (1.0 - jnp.sum(pi * pi, axis=1, keepdims=True))
    lengths = lengths_ref[...]
    r = jnp.exp(beta * lengths) - 1.0
    drift = beta * jnp.sum(lengths, axis=1, keepdims=True)

    table[...] = jnp.zeros_like(table)
    hi = r.astype(bf16).astype(f32)
    rest = r - hi
    mid = rest.astype(bf16).astype(f32)
    table[0:classes, 0:branches] = hi
    table[classes : 2 * classes, 0:branches] = mid
    table[2 * classes : 3 * classes, 0:branches] = rest - mid
    kids = kids_ref[...]
    table[12:14, taxa : taxa + kids.shape[1]] = (kids >> 8).astype(f32)
    table[14:16, taxa : taxa + kids.shape[1]] = (kids & 255).astype(f32)

    pi8 = jnp.concatenate([pi] * halves, axis=0)
    for c in range(classes):
        for i in range(4):
            wide = jnp.broadcast_to(pi[:, i : i + 1], (classes, LANES))
            stat[c, i] = jnp.broadcast_to(wide[c : c + 1], (8, LANES))
    first_up = level_base(taxa, low)
    window = first_up // LANES * LANES
    r8 = jnp.concatenate([r[:, window:branches]] * halves, axis=0)
    for j in range(branches - first_up):
        at = first_up - window + j
        grow_up[j] = jnp.broadcast_to(r8[:, at : at + 1], (rows, LANES))

    q = lax.broadcasted_iota(jnp.int32, (1, local), 1)
    ancestor = (first_up + g * clades + (q & (clades - 1))).astype(f32)
    offset = {}
    total_rows = 0
    for h in range(low):
        offset[h] = total_rows
        total_rows += local >> h
    for h in range(low, -1, -1):
        count = local >> h
        base = level_base(taxa, h)
        if count % LANES == 0:
            start = pl.multiple_of(base + g * count, LANES)
            width = count
        else:
            start = base // LANES * LANES
            end = base + (taxa >> h)
            width = -(-end // LANES) * LANES - start
        ids = lax.broadcasted_iota(jnp.int32, (width, local), 0) + start
        onehot = (ids.astype(f32) == ancestor).astype(f32).astype(bf16)
        part_table = table[:, pl.ds(start, width)].astype(bf16)
        out = jnp.dot(part_table, onehot, preferred_element_type=f32)
        if h < low:
            r_row = out[0:classes] + out[classes : 2 * classes] + out[2 * classes : 3 * classes]
            r_col = jnp.concatenate([r_row, r_row], axis=0).T
            for c in range(classes):
                grow[c, offset[h] : offset[h] + count, :] = jnp.broadcast_to(
                    r_col[:count, c : c + 1], (count, LANES)
                )
        if h > 0:
            left = out[12:13] * 256.0 + out[14:15]
            right = out[13:14] * 256.0 + out[15:16]
            ancestor = jnp.where((q & count) != 0, right, left)
    tip_col = jnp.broadcast_to(ancestor, (8, local)).T[:, 0:1]
    tip_ids = (lax.broadcasted_iota(jnp.int32, (local, local), 1) + g * local).astype(f32)
    order = (tip_ids == tip_col).astype(f32).astype(bf16)

    fetch.wait()

    def quarter_of(k, dest):
        block = lax.rem(g + k, groups)
        for half in range(halves):
            lanes = pl.ds(pl.multiple_of(block * quarter + half * LANES, LANES), LANES)
            picked[half] = jnp.dot(
                order, codes[:, lanes].astype(f32).astype(bf16), preferred_element_type=f32
            )

        def one(step, carry):
            half = step // (classes // 2)
            pair = lax.rem(step, classes // 2) * 2
            both = (0, 1)
            pis = [[stat[pair + b, i] for i in range(4)] for b in both]

            def factor(b, h, n):
                return grow[pair + b, offset[h] + 8 * n : offset[h] + 8 * n + 8, :]

            def tip(n):
                code = picked[half, 8 * n : 8 * n + 8, :]
                marks = [code == float(i) for i in range(4)]
                result = []
                for b in both:
                    own = jnp.where(marks[2], pis[b][2], pis[b][3])
                    own = jnp.where(marks[0], pis[b][0], jnp.where(marks[1], pis[b][1], own))
                    off = factor(b, 0, n) * own
                    on = off + 1.0
                    result.append([jnp.where(mark, on, off) for mark in marks])
                return result

            def spread(b, values, scale):
                mean = (values[0] * pis[b][0] + values[1] * pis[b][1]) + (
                    values[2] * pis[b][2] + values[3] * pis[b][3]
                )
                move = scale * mean
                return [value + move for value in values]

            logs = ([], [])

            def node(h, n):
                if h == 0:
                    return tip(n)
                gap = (local >> h) // 8
                left = node(h - 1, n)
                right = node(h - 1, n + gap)
                result = []
                for b in both:
                    one_left, one_right = left[b], right[b]
                    if h > 1:
                        one_left = spread(b, one_left, factor(b, h - 1, n))
                        one_right = spread(b, one_right, factor(b, h - 1, n + gap))
                    values = [x * y for x, y in zip(one_left, one_right)]
                    if h == 3:
                        largest = jnp.maximum(
                            jnp.maximum(values[0], values[1]), jnp.maximum(values[2], values[3])
                        )
                        scale = pl.reciprocal(largest, approx=True)
                        logs[b].append(jnp.log(scale))
                        values = [value * scale for value in values]
                    result.append(values)
                return result

            ends = node(low - 1, 0)
            for b in both:
                row = pl.ds(half * classes + pair + b, 1)
                values = spread(b, ends[b], factor(b, low - 1, 0))
                values = [value[0:clades] * value[clades : 2 * clades] for value in values]
                log_sum = jnp.sum(sum(logs[b][1:], logs[b][0]), axis=0, keepdims=True)
                log_sum = jnp.sum(jnp.log(values[3]), axis=0, keepdims=True) - log_sum
                inverse = 1.0 / values[3]
                for i in range(3):
                    ratio = values[i] * inverse
                    for j in range(clades):
                        dest[j * 3 + i, row, :] = ratio[j : j + 1]
                dest[clades * 3, row, :] = log_sum
            return carry

        lax.fori_loop(0, rows // 2, one, 0)

    copies = []
    for place, k in enumerate([2, 1, 3] if groups == 4 else range(1, groups)):
        quarter_of(k, sent.at[k])
        if place == 0:
            pl.semaphore_wait(barrier, groups + site_devices - 2)
        copy = pltpu.make_async_remote_copy(
            src_ref=sent.at[k],
            dst_ref=got.at[k],
            send_sem=send_sem.at[k],
            recv_sem=recv_sem.at[k],
            device_id={"cls": lax.rem(g + k, groups)},
            device_id_type=MESH,
        )
        copy.start()
        copies.append(copy)
    quarter_of(0, got.at[0])
    for copy in copies:
        copy.wait()

    pis8 = [jnp.broadcast_to(pi8[:, i : i + 1], (rows, LANES)) for i in range(4)]
    scales = got[0, clades * 3]
    for k in range(1, groups):
        scales = scales + got[k, clades * 3]

    def child(tree_level, ident):
        if tree_level == low:
            clade = jnp.clip(ident - first_up, 0, 2**TOP - 1)
            k = lax.rem(g + groups - clade // clades, groups)
            row = lax.rem(clade, clades) * 3
            values = [got[k, row + i] for i in range(3)] + [jnp.ones((rows, LANES), f32)]
        else:
            at = jnp.clip(ident - level_base(taxa, low + 1), 0, 2**TOP - 1)
            values = [upper[at, i] for i in range(4)]
        mean = (values[0] * pis8[0] + values[1] * pis8[1]) + (
            values[2] * pis8[2] + values[3] * pis8[3]
        )
        move = grow_up[jnp.clip(ident - first_up, 0, branches - first_up - 1)] * mean
        return [value + move for value in values]

    place = 0
    for tree_level in range(low, LEVELS):
        count = taxa >> (tree_level + 1)
        first = taxa - (taxa >> tree_level)
        for n in range(count):
            left = child(tree_level, kids_smem[0, first + n])
            right = child(tree_level, kids_smem[1, first + n])
            values = [a * b for a, b in zip(left, right)]
            largest = jnp.maximum(
                jnp.maximum(values[0], values[1]), jnp.maximum(values[2], values[3])
            )
            scale = pl.reciprocal(largest, approx=True)
            scales = scales - jnp.log(scale)
            values = [value * scale for value in values]
            if tree_level < LEVELS - 1:
                for i in range(4):
                    upper[place, i] = values[i]
                place += 1
    end = (values[0] * pis8[0] + values[1] * pis8[1]) + (
        values[2] * pis8[2] + values[3] * pis8[3]
    )
    spot = lax.broadcasted_iota(jnp.int32, (classes, classes), 0)
    spot = spot == lax.broadcasted_iota(jnp.int32, (classes, classes), 1)
    weights = jnp.sum(jnp.where(spot, weights_ref[...], 0.0), axis=1, keepdims=True)
    log_weight = jnp.log(weights / jnp.sum(weights, axis=0, keepdims=True))
    bias = jnp.concatenate([log_weight - drift] * halves, axis=0)
    shifted = scales + jnp.log(end) + bias

    mass = jnp.zeros((classes, LANES), f32)
    loglik = jnp.zeros((1, LANES), f32)
    seen = jnp.zeros((1, LANES), f32)
    for half in range(halves):
        a = shifted[half * classes : (half + 1) * classes]
        top = jnp.max(a, axis=0, keepdims=True)
        total = top + jnp.log(jnp.sum(jnp.exp(a - top), axis=0, keepdims=True))
        n = counts_ref[pl.ds(g * halves + half, 1), :].astype(f32)
        result[half : half + 1, :] = total / taxa
        mass = mass + n * jnp.exp(a - total)
        loglik = loglik + n * total
        seen = seen + n
    part[...] = jnp.zeros_like(part)
    part[0:classes] = mass
    part[classes : classes + 1] = loglik
    part[classes + 1 : classes + 2] = seen

    copies = []
    for k in range(1, groups):
        copy = pltpu.make_async_remote_copy(
            src_ref=part,
            dst_ref=part_got.at[k],
            send_sem=part_send.at[k],
            recv_sem=part_recv.at[k],
            device_id={"cls": lax.rem(g + k, groups)},
            device_id_type=MESH,
        )
        copy.start()
        copies.append(copy)
    for copy in copies:
        copy.wait()
    part_got[0] = part[...]
    sums = part_got[lax.rem(g + groups, groups)]
    for d in range(1, groups):
        sums = sums + part_got[lax.rem(g + groups - d, groups)]
    group_sum[...] = sums
    copies = []
    for k in range(1, site_devices):
        copy = pltpu.make_async_remote_copy(
            src_ref=group_sum,
            dst_ref=group_got.at[k],
            send_sem=sum_send.at[k],
            recv_sem=sum_recv.at[k],
            device_id={"site": lax.rem(me + k, site_devices)},
            device_id_type=MESH,
        )
        copy.start()
        copies.append(copy)
    for copy in copies:
        copy.wait()
    group_got[0] = sums
    sums = group_got[lax.rem(me + site_devices, site_devices)]
    for d in range(1, site_devices):
        sums = sums + group_got[lax.rem(me + site_devices - d, site_devices)]
    line = jnp.sum(sums, axis=1, keepdims=True)
    all_count = line[classes + 1 : classes + 2]
    mean = line[classes : classes + 1] / (all_count * taxa)
    share = line[0:classes] / all_count
    mine = lax.broadcasted_iota(jnp.int32, (classes, 1), 0) == g
    share = jnp.sum(jnp.where(mine, share, 0.0), axis=0, keepdims=True)
    result[halves : halves + 1, :] = jnp.broadcast_to(share, (1, LANES))
    result[halves + 1 : halves + 2, :] = jnp.broadcast_to(mean, (1, LANES))


def finish(result, site_out, weight_out, mean_out):
    halves = result.shape[0] - 2
    for half in range(halves):
        site_out[0:1, half * LANES : (half + 1) * LANES] = result[half : half + 1, :]
    weight_out[...] = result[halves : halves + 1, 0:1]
    mean_out[...] = result[halves + 1 : halves + 2, 0:1]


def solution(mesh):
    groups = mesh.shape["cls"]
    site_devices = mesh.shape["site"]

    def per_device(tip_codes, counts, children, lengths, frequencies, weights):
        local, sites = tip_codes.shape
        taxa = local * groups
        classes, branches = lengths.shape
        quarter = sites // groups
        halves = quarter // LANES
        rows = halves * classes
        low = LEVELS - TOP
        clades = local >> low
        low_rows = sum(local >> h for h in range(low))
        table_width = -(-(branches + 1) // LANES) * LANES
        up_count = branches - level_base(taxa, low)
        kids = children.T
        vmem = pl.BlockSpec(memory_space=pltpu.VMEM)
        smem = pl.BlockSpec(memory_space=pltpu.SMEM)
        f32 = jnp.float32
        result = pl.pallas_call(
            functools.partial(kernel, groups, site_devices),
            out_shape=jax.ShapeDtypeStruct((halves + 2, LANES), f32),
            in_specs=[pl.BlockSpec(memory_space=pl.ANY), vmem, vmem, smem, vmem, vmem, vmem],
            out_specs=vmem,
            scratch_shapes=[
                pltpu.VMEM((local, sites), jnp.int32),
                pltpu.VMEM((halves, local, LANES), f32),
                pltpu.VMEM((16, table_width), f32),
                pltpu.VMEM((classes, low_rows, LANES), f32),
                pltpu.VMEM((up_count, rows, LANES), f32),
                pltpu.VMEM((classes, 4, 8, LANES), f32),
                pltpu.VMEM((groups, clades * 3 + 1, rows, LANES), f32),
                pltpu.VMEM((groups, clades * 3 + 1, rows, LANES), f32),
                pltpu.VMEM((2 ** TOP, 4, rows, LANES), f32),
                pltpu.VMEM((8, LANES), f32),
                pltpu.VMEM((groups, 8, LANES), f32),
                pltpu.VMEM((8, LANES), f32),
                pltpu.VMEM((site_devices, 8, LANES), f32),
                pltpu.SemaphoreType.DMA,
                pltpu.SemaphoreType.DMA((groups,)),
                pltpu.SemaphoreType.DMA((groups,)),
                pltpu.SemaphoreType.DMA((groups,)),
                pltpu.SemaphoreType.DMA((groups,)),
                pltpu.SemaphoreType.DMA((site_devices,)),
                pltpu.SemaphoreType.DMA((site_devices,)),
            ],
            compiler_params=pltpu.CompilerParams(collective_id=0, has_side_effects=True),
        )(
            tip_codes,
            counts.reshape(sites // LANES, LANES),
            kids,
            kids,
            lengths,
            frequencies,
            weights.reshape(1, classes),
        )
        site_loglik, new_weights, mean_loglik = pl.pallas_call(
            finish,
            out_shape=(
                jax.ShapeDtypeStruct((1, quarter), f32),
                jax.ShapeDtypeStruct((1, 1), f32),
                jax.ShapeDtypeStruct((1, 1), f32),
            ),
            in_specs=[vmem],
            out_specs=(vmem, vmem, vmem),
        )(result)
        return site_loglik, new_weights.reshape(1), mean_loglik.reshape(())

    return jax.shard_map(
        per_device,
        mesh=mesh,
        in_specs=(P("cls", "site"), P("site"), P(), P(), P(), P()),
        out_specs=(P("cls", "site"), P("cls"), P()),
        check_vma=False,
    )
```
